256 devices in a mesh: seq: 16 (over z, core), mp: 8 (over y, x_hi), dp: 2 (over x_lo).
Axes of the slice: x: 4 (x_hi: 2, x_lo: 2; x = x_hi * 2 + x_lo), y: 4, z: 8, core: 2. Of those that a mesh axis runs over, the one named last changes fastest.
Arguments:
- latents: bfloat16 [2, 3072, 1792], P('dp', 'seq', 'mp'), may hold values from -6 to 6
- grad_out: bfloat16 [2, 3072, 1792], P('dp', 'seq', 'mp'), may hold values from -6 to 6
- sync_mod: bfloat16 [2, 2400, 3584], P('dp', 'seq'), may hold values from -3 to 3
- w_qkv: bfloat16 [1792, 3, 1024], P(None, None, 'mp'), may hold values from -0.125 to 0.125
- w_out: bfloat16 [1024, 1792], P('mp'), may hold values from -0.1875 to 0.1875
- q_gain: float32 [8, 128], P('mp'), may hold values from 0.5 to 2.5
- k_gain: float32 [8, 128], P('mp'), may hold values from 0.5 to 2.5
- frame_of: int32 [2, 3072], P('dp', 'seq'), may hold values from 0 to 2399, as said below
- group_id: int32 [2, 3072], P('dp'), may hold values from 0 to 63, never falling along the last dimension, each value on 1 to 96 neighbouring positions
- clip_len: int32 [2], P('dp'), may hold values from 1536 to 3072
Outputs:
- mixed: bfloat16 [2, 3072, 1792], P('dp', 'seq', 'mp')
- grad_latents: bfloat16 [2, 3072, 1792], P('dp', 'seq', 'mp')
- grad_wqkv: float32 [1792, 3, 1024], P(('seq', 'dp'), None, 'mp')
- grad_wout: float32 [1024, 1792], P('mp', ('seq', 'dp'))
The draws below stay inside these ranges and needn't reach their ends.
Inputs may be any that keep to these rules, and one draw needn't show every extreme that they name: frame_of[c, l] = floor((96 l + s) / 125) with a phase s of 0 to 124 drawn for each clip, so the latents on seq index j read frames held by seq indices j - 1 and j only.
All inputs are finite; a program needn't handle non-finite values.
Results may differ from the reference program's by a relative error of at most 0.012.
The reference program's roundings to bfloat16 on the way (of `hidden`, `query_norm`, `heads_out`, `grad_heads`, `grad_logits` and `grad_proj`) count: a program that leaves them out, or rounds other values in their place, can miss the bound.
Values may be sent and summed in bfloat16 or wider, within the bound.
A program may use at most 64 MiB of HBM per device.

```python
import math
import jax
import jax.numpy as jnp
import numpy as np
from jax import lax

D = 1792
HEADS = 8
HD = 128
GROUP = 96
CLIPS = 2
LATENTS = 3072
FRAMES = 2400
GROUPS = 64


def draw_q_gain(key, part):
    sub_key = jax.random.fold_in(key, 11)
    return jax.random.uniform(sub_key, (HEADS, HD), jnp.float32, 0.5, 1.6)


def draw_k_gain(key, part):
    sub_key = jax.random.fold_in(key, 12)
    return jax.random.uniform(sub_key, (HEADS, HD), jnp.float32, 0.5, 1.6)


def draw_frame_of(key, part):
    phases = jax.random.randint(jax.random.fold_in(key, 21), (CLIPS, 1), 0, 125, dtype=jnp.int32)
    positions = lax.iota(jnp.int32, LATENTS)[None, :]
    return ((96 * positions + phases) // 125).astype(jnp.int32)


def steps_of(rng, extent, pieces, least, largest):
    def one(axis_at, shards_of):
        steps = jax.random.uniform(jax.random.fold_in(jax.random.fold_in(rng, 6), axis_at), (shards_of,), jnp.float32, least / len(pieces), largest / len(pieces))
        return jnp.repeat(jnp.exp(steps), extent[axis_at] // shards_of).reshape((-1,) + (1,) * (len(extent) - axis_at - 1))

    level = one(*pieces[0])
    for cut in pieces[1:]:
        level = level * one(*cut)
    return level


def split_up(amount, total, reach, skew):
    loads = [(1 << 20) // math.isqrt(rank ** skew) + 1 for rank in range(2, amount + 1)]
    spare, holding = total - reach - (amount - 1), [1] * (amount - 1)
    while spare > 0:
        free = [i for i in range(amount - 1) if holding[i] < reach]
        pool, budget = sum([loads[i] for i in free]), spare
        for i in free:
            addition = min(reach - holding[i], max(1, budget * loads[i] // pool), spare)
            holding[i] = holding[i] + addition
            spare = spare - addition
    return np.array([reach] + holding)


def ragged(rng, number_of, total, reach, skew):
    if number_of == 2:
        one = jax.random.randint(rng, (), max(1, total - reach), min(reach, total - 1) + 1)
        return jnp.stack([one, total - one])
    tallies = jnp.asarray(split_up(number_of, total, reach, skew), jnp.int32)
    couples = (number_of - 1) // 2
    giver, taker = tallies[1:1 + 2 * couples:2], tallies[2:2 + 2 * couples:2]
    room = jnp.minimum(giver - 1, reach - taker)
    passed = jax.random.randint(jax.random.fold_in(rng, 1), (couples,), 0, 1 << 20) % (room + 1)
    tallies = tallies.at[1:1 + 2 * couples:2].set(giver - passed).at[2:2 + 2 * couples:2].set(taker + passed)
    return tallies[jax.random.permutation(jax.random.fold_in(rng, 2), number_of)]


def centred(rng, dims, scale, reach, cuts=(), kind=jnp.bfloat16):
    level = steps_of(rng, dims, cuts, -0.22, 0.18) if cuts else 1.0
    entries = jax.random.normal(rng, dims, jnp.float32) * scale * level
    return jnp.minimum(jnp.maximum(entries, -reach), reach).astype(kind)


def setup_inputs(seed: int = 0) -> dict:
    keys = jax.random.split(jax.random.key(seed), 11)
    latents = centred(keys[0], (CLIPS, LATENTS, D), 1.0, 6.0, ((0, 2), (1, 16), (2, 8)))
    grad_out = centred(keys[1], (CLIPS, LATENTS, D), 1.0, 6.0, ((0, 2), (1, 16), (2, 8)))
    sync_mod = centred(keys[2], (CLIPS, FRAMES, 2 * D), 0.5, 3.0, ((0, 2), (1, 16)))
    w_qkv = centred(keys[3], (D, 3, HEADS * HD), D ** -0.5, 0.125, ((2, 8),))
    w_out = centred(keys[4], (HEADS * HD, D), (HEADS * HD) ** -0.5, 0.1875, ((0, 8),))
    q_gain = draw_q_gain(jax.random.fold_in(keys[10], 71), 0)
    k_gain = draw_k_gain(jax.random.fold_in(keys[10], 71), 0)
    frame_of = draw_frame_of(jax.random.fold_in(keys[10], 71), 0)
    group_id = jax.vmap(lambda own: jnp.searchsorted(jnp.cumsum(ragged(own, GROUPS, LATENTS, GROUP, 1)), jnp.arange(LATENTS), side="right"))(jax.random.split(keys[8], CLIPS)).reshape((CLIPS, LATENTS)).astype(jnp.int32)
    clip_len = jax.random.randint(keys[9], (CLIPS,), LATENTS // 2, LATENTS + 1).astype(jnp.int32)
    return dict(latents=latents, grad_out=grad_out, sync_mod=sync_mod, w_qkv=w_qkv, w_out=w_out, q_gain=q_gain, k_gain=k_gain, frame_of=frame_of, group_id=group_id, clip_len=clip_len)


EPSILON = 1e-06
NEG_FILL = -1e+30

def inv_rms(values):
    return lax.rsqrt(lax.optimization_barrier(jnp.mean(values * values, axis=-1, keepdims=True)) + EPSILON)

def rounded(values):
    return lax.optimization_barrier(values.astype(jnp.bfloat16)).astype(jnp.float32)

def norm_back(raw, inv_norm, gains, upstream):
    inner_dot = lax.optimization_barrier(jnp.mean(upstream * gains * raw, axis=-1, keepdims=True))
    return inv_norm * (gains * upstream - raw * inv_norm * inv_norm * inner_dot)

def clip_attention(operands):
    query_norm, key_norm, values, grad_heads, group_ids, clip_length = operands
    seq_length = query_norm.shape[0]
    factor = query_norm.shape[-1] ** (-0.5)
    positions = lax.iota(jnp.int32, seq_length)
    allowed = ((group_ids[None, :] <= group_ids[:, None]) & (positions[None, :] < clip_length))[None]
    query_f = query_norm.astype(jnp.float32)
    key_f = key_norm.astype(jnp.float32)
    value_f = values.astype(jnp.float32)
    logits = jnp.einsum('qhd,khd->hqk', query_f, key_f) * factor
    logits = jnp.where(allowed, logits, NEG_FILL)
    row_max = lax.optimization_barrier(jnp.max(logits, axis=-1, keepdims=True))
    unnorm = jnp.where(allowed, jnp.exp(logits - row_max), 0.0)
    row_sum = lax.optimization_barrier(jnp.sum(unnorm, axis=-1, keepdims=True))
    heads_out = jnp.einsum('hqk,khd->qhd', rounded(unnorm), value_f) / jnp.transpose(row_sum, (1, 0, 2))
    heads_out = heads_out.astype(jnp.bfloat16)
    upstream = grad_heads.astype(jnp.float32)
    out_dot = lax.optimization_barrier(jnp.sum(upstream * heads_out.astype(jnp.float32), axis=-1))
    probs = unnorm / row_sum
    grad_probs = jnp.einsum('qhd,khd->hqk', upstream, value_f)
    grad_logits = rounded(probs * (grad_probs - jnp.transpose(out_dot)[:, :, None]))
    grad_query = jnp.einsum('hqk,khd->qhd', grad_logits, key_f) * factor
    grad_key = jnp.einsum('hqk,qhd->khd', grad_logits, query_f) * factor
    grad_value = jnp.einsum('hqk,qhd->khd', rounded(probs), upstream)
    return (heads_out, grad_query, grad_key, grad_value)

def reference(latents, grad_out, sync_mod, w_qkv, w_out, q_gain, k_gain, frame_of, group_id, clip_len):
    clip_count, seq_length, model_width = latents.shape
    heads_all, head_dim = q_gain.shape
    inner_width = heads_all * head_dim
    inputs_f = latents.astype(jnp.float32)
    inv_norm = inv_rms(inputs_f)
    normed = inputs_f * inv_norm
    modulation = jax.vmap(lambda lookup_table, row_index: lookup_table[row_index])(sync_mod, frame_of).astype(jnp.float32)
    mod_scale = modulation[:, :, :model_width]
    mod_gate = modulation[:, :, model_width:]
    hidden = (normed * (1.0 + mod_scale)).astype(jnp.bfloat16)
    flat_hidden = hidden.reshape(clip_count * seq_length, model_width)
    flat_weight = w_qkv.reshape(model_width, 3 * inner_width)
    projected = jnp.dot(flat_hidden, flat_weight, preferred_element_type=jnp.float32)
    projected = projected.reshape(clip_count, seq_length, 3, heads_all, head_dim)
    query_raw = projected[:, :, 0]
    key_raw = projected[:, :, 1]
    query_inv = inv_rms(query_raw)
    key_inv = inv_rms(key_raw)
    query_norm = (query_raw * query_inv * q_gain).astype(jnp.bfloat16)
    key_norm = (key_raw * key_inv * k_gain).astype(jnp.bfloat16)
    values = projected[:, :, 2].astype(jnp.bfloat16)
    grad_attn = (grad_out.astype(jnp.float32) * mod_gate).astype(jnp.bfloat16)
    flat_grad = grad_attn.reshape(clip_count * seq_length, model_width)
    grad_heads = jnp.dot(flat_grad, w_out.T, preferred_element_type=jnp.float32).astype(jnp.bfloat16)
    grad_heads = grad_heads.reshape(clip_count, seq_length, heads_all, head_dim)
    heads_out, grad_qnorm, grad_knorm, grad_values = lax.map(clip_attention, (query_norm, key_norm, values, grad_heads, group_id, clip_len))
    out_rows = heads_out.reshape(clip_count * seq_length, inner_width)
    attn = jnp.dot(out_rows, w_out, preferred_element_type=jnp.float32).reshape(clip_count, seq_length, model_width)
    mixed = (inputs_f + mod_gate * attn).astype(jnp.bfloat16)
    grad_wout = jnp.dot(out_rows.T, flat_grad, preferred_element_type=jnp.float32)
    grad_query = norm_back(query_raw, query_inv, q_gain, grad_qnorm)
    grad_key = norm_back(key_raw, key_inv, k_gain, grad_knorm)
    grad_proj = jnp.stack([grad_query, grad_key, grad_values], axis=2).astype(jnp.bfloat16)
    grad_proj = grad_proj.reshape(clip_count * seq_length, 3 * inner_width)
    grad_wqkv = jnp.dot(flat_hidden.T, grad_proj, preferred_element_type=jnp.float32).reshape(model_width, 3, inner_width)
    grad_hidden = jnp.dot(grad_proj, flat_weight.T, preferred_element_type=jnp.float32).reshape(clip_count, seq_length, model_width)
    grad_normed = grad_hidden * (1.0 + mod_scale)
    grad_inputs = inv_norm * (grad_normed - normed * lax.optimization_barrier(jnp.mean(grad_normed * normed, axis=-1, keepdims=True)))
    grad_latents = (grad_out.astype(jnp.float32) + grad_inputs).astype(jnp.bfloat16)
    return (mixed, grad_latents, grad_wqkv, grad_wout)
```

```python
import functools

import jax
import jax.numpy as jnp
from jax import lax
from jax.experimental import pallas as pl
from jax.experimental.pallas import tpu as pltpu
from jax.sharding import PartitionSpec as P

EPSILON = 1e-06
NEG_FILL = -1e30
TAIL = 48

F32 = jnp.float32
BF16 = jnp.bfloat16
MESH = pl.DeviceIdType.MESH


def dot_nn(a, b):
    return lax.dot_general(a, b, (((1,), (0,)), ((), ())), preferred_element_type=F32)


def dot_nt(a, b):
    return lax.dot_general(a, b, (((1,), (1,)), ((), ())), preferred_element_type=F32)


def dot_tn(a, b):
    return lax.dot_general(a, b, (((0,), (0,)), ((), ())), preferred_element_type=F32)


def norm_back(raw, inv_norm, gains, upstream):
    inner_dot = jnp.mean(upstream * gains * raw, axis=-1, keepdims=True)
    return inv_norm * (gains * upstream - raw * inv_norm * inv_norm * inner_dot)


def send(src, dst, send_sem, recv_sem, where):
    pltpu.make_async_remote_copy(
        src_ref=src, dst_ref=dst, send_sem=send_sem, recv_sem=recv_sem,
        device_id=where, device_id_type=MESH,
    ).start()


def arrived(dst, send_sem, recv_sem, where):
    pltpu.make_async_remote_copy(
        src_ref=dst, dst_ref=dst, send_sem=send_sem, recv_sem=recv_sem,
        device_id=where, device_id_type=MESH,
    ).wait_recv()


def drained(src, send_sem, recv_sem, where):
    pltpu.make_async_remote_copy(
        src_ref=src, dst_ref=src, send_sem=send_sem, recv_sem=recv_sem,
        device_id=where, device_id_type=MESH,
    ).wait_send()


def block_kernel(
    sizes,
    lat_ref, go_ref, win_ref, tail_ref, wq_ref, wo_ref, qg_ref, kg_ref, frame_ref, group_ref, len_ref,
    mixed_ref, gl_ref, gwq_ref, gwo_ref,
    prev, ga_all, hid_all, ssq_all, kv_all, qo_all, p_all, stats_all, ho_all, wo_recv,
    gh_send, gh_recv, dot_all, cx_send, cx_recv, half, dx_send, dx_recv, quarter, zs_send, zs_recv,
    proj, scale_s, gate_s, normed_s, go_acc, mx_s, rs_s, acc_s, dk_s, dv_s, gw_s,
    prev_sem, ga_ss, ga_rs, hid_ss, hid_rs, ssq_ss, ssq_rs, kv_ss, kv_fs, kv_rs, qo_ss, qo_fs, qo_rs,
    st_ss, st_rs, ho_ss, ho_rs, wo_ss, wo_rs, gh_ss, gh_rs, dot_ss, dot_rs, cx_ss, cx_rs, dx_ss, dx_rs,
    zs_ss, zs_rs,
):
    S, M, frames = sizes
    Z = S // 2
    rows, width = lat_ref.shape
    hd = qg_ref.shape[1]
    factor = hd ** (-0.5)
    piece = width // 4
    s = lax.axis_index("seq")
    m = lax.axis_index("mp")
    d = lax.axis_index("dp")
    z, c = lax.div(s, 2), lax.rem(s, 2)
    mate = z * 2 + 1 - c
    other_d = 1 - d

    barrier = pltpu.get_barrier_semaphore()
    for k in range(1, M):
        pl.semaphore_signal(barrier, inc=1, device_id={"mp": lax.rem(m + k, M)}, device_id_type=MESH)
    for k in range(1, S):
        pl.semaphore_signal(barrier, inc=1, device_id={"seq": lax.rem(s + k, S)}, device_id_type=MESH)
    pl.semaphore_signal(barrier, inc=1, device_id={"dp": other_d}, device_id_type=MESH)

    eye = lax.broadcasted_iota(jnp.int32, (rows, rows), 0) == lax.broadcasted_iota(jnp.int32, (rows, rows), 1)

    def to_row(col):
        return jnp.sum(jnp.where(eye, jnp.broadcast_to(col, (rows, rows)), 0.0), axis=0, keepdims=True)

    def to_col(row):
        return jnp.sum(jnp.where(eye, jnp.broadcast_to(row, (rows, rows)), 0.0), axis=1, keepdims=True)

    lat = lat_ref[...].astype(F32)
    ssq = to_row(jnp.sum(lat * lat, axis=1, keepdims=True))
    ssq_all[m] = jnp.broadcast_to(ssq, (8, rows))
    local_frame = frame_ref[...] - frames * s
    own_rows = win_ref.shape[0]
    pick_own = jnp.where(
        lax.broadcasted_iota(jnp.int32, (own_rows, rows), 0) == local_frame, 1.0, 0.0
    ).astype(BF16)
    pick_prev = jnp.where(
        lax.broadcasted_iota(jnp.int32, (TAIL, rows), 0) == local_frame + TAIL, 1.0, 0.0
    ).astype(BF16)
    mod_own = dot_tn(pick_own, win_ref[...])

    pl.semaphore_wait(barrier, (M - 1) + (S - 1) + 1)

    after = {"seq": lax.rem(s + 1, S)}
    send(tail_ref, prev, prev_sem.at[0], prev_sem.at[1], after)
    for k in range(1, M):
        to = lax.rem(m + k, M)
        send(ssq_all.at[m], ssq_all.at[m], ssq_ss.at[to], ssq_rs.at[m], {"mp": to})

    arrived(prev, prev_sem.at[0], prev_sem.at[1], after)
    modulation = mod_own + dot_tn(pick_prev, prev[...])
    scale = modulation[:, :width]
    gate = modulation[:, 256:256 + width]
    scale_s[...] = scale
    gate_s[...] = gate
    ga_all[m] = (go_ref[...].astype(F32) * gate).astype(BF16)
    for k in range(1, M):
        to = lax.rem(m + k, M)
        send(ga_all.at[m], ga_all.at[m], ga_ss.at[to], ga_rs.at[m], {"mp": to})

    for k in range(1, M):
        at = lax.rem(m + k, M)
        arrived(ssq_all.at[at], ssq_ss.at[at], ssq_rs.at[at], {"mp": at})
    total = ssq_all[0, 0:1, :]
    for k in range(1, M):
        total = total + ssq_all[k, 0:1, :]
    inv_col = to_col(lax.rsqrt(total * (1.0 / (M * width)) + EPSILON))
    normed = lat * inv_col
    normed_s[...] = normed
    hid_all[m] = (normed * (1.0 + scale)).astype(BF16)
    for k in range(1, M):
        to = lax.rem(m + k, M)
        send(hid_all.at[m], hid_all.at[m], hid_ss.at[to], hid_rs.at[m], {"mp": to})
    for k in range(1, M):
        to = lax.rem(m + k, M)
        send(wo_ref.at[to], wo_recv.at[m], wo_ss.at[to], wo_rs.at[m], {"mp": to})
    wo_recv[m] = wo_ref[m]

    go_acc[...] = dot_nt(ga_all[m], wo_ref[m])

    def take_ga(k, carry):
        at = lax.rem(m + k, M)
        arrived(ga_all.at[at], ga_ss.at[at], ga_rs.at[at], {"mp": at})
        go_acc[...] += dot_nt(ga_all[at], wo_ref[at])
        return carry

    lax.fori_loop(1, M, take_ga, 0)
    proj[...] = dot_nn(hid_all[m], wq_ref[m])

    def take_hid(k, carry):
        at = lax.rem(m + k, M)
        arrived(hid_all.at[at], hid_ss.at[at], hid_rs.at[at], {"mp": at})
        proj[...] += dot_nn(hid_all[at], wq_ref[at])
        return carry

    lax.fori_loop(1, M, take_hid, 0)
    q_gain, k_gain = qg_ref[...], kg_ref[...]
    query_raw, key_raw = proj[:, :hd], proj[:, hd:2 * hd]
    query_inv = lax.rsqrt(jnp.mean(query_raw * query_raw, axis=-1, keepdims=True) + EPSILON)
    key_inv = lax.rsqrt(jnp.mean(key_raw * key_raw, axis=-1, keepdims=True) + EPSILON)
    kv_all[s, :, :hd] = (key_raw * key_inv * k_gain).astype(BF16)
    kv_all[s, :, hd:] = proj[:, 2 * hd:].astype(BF16)
    qo_all[s, :, :hd] = (query_raw * query_inv * q_gain).astype(BF16)
    qo_all[s, :, hd:] = go_acc[...].astype(BF16)

    def kv_to(t):
        send(kv_all.at[s], kv_all.at[s], kv_ss.at[t], kv_rs.at[s], {"seq": t})

    def qo_to(t):
        send(qo_all.at[s], qo_all.at[s], qo_ss.at[t], qo_rs.at[s], {"seq": t})

    kv_bound = (c == 0) & (z > 0)
    qo_bound = (c == 1) & (z < Z - 1)
    kv_to(mate)
    qo_to(mate)
    for k in range(1, Z):
        @pl.when(z + k < Z)
        def _():
            kv_to(s + 2 * k)

        @pl.when(z - k >= 0)
        def _():
            qo_to(s - 2 * k)

        if k == 1:
            @pl.when(kv_bound)
            def _():
                kv_to(s - 1)

            @pl.when(qo_bound)
            def _():
                qo_to(s + 1)

    own_group = to_col(group_ref[s].astype(F32))
    clip_length = len_ref[0]
    query = qo_all[s, :, :hd]
    upstream = qo_all[s, :, hd:]
    mx_s[...] = jnp.full_like(mx_s, NEG_FILL)

    def score(t):
        key_place = t * rows + lax.broadcasted_iota(jnp.int32, (1, rows), 1)
        allowed = (group_ref[t].astype(F32) <= own_group) & (key_place < clip_length)
        logits = dot_nt(qo_all[s, :, :hd], kv_all[t, :, :hd]) * factor
        logits = jnp.where(allowed, logits, NEG_FILL)
        p_all[t] = logits
        mx_s[...] = jnp.maximum(mx_s[...], jnp.max(logits, axis=-1, keepdims=True))

    def wait_kv(t):
        arrived(kv_all.at[t], kv_fs.at[t], kv_rs.at[t], {"seq": mate})

    def wait_qo(t):
        arrived(qo_all.at[t], qo_fs.at[t], qo_rs.at[t], {"seq": mate})

    score(s)
    wait_kv(mate)
    score(mate)

    def take_direct(k, carry):
        @pl.when(z - k >= 0)
        def _():
            t = s - 2 * k
            wait_kv(t)
            send(kv_all.at[t], kv_all.at[t], kv_fs.at[t], kv_rs.at[t], {"seq": mate})

        @pl.when(z + k < Z)
        def _():
            t = s + 2 * k
            wait_qo(t)
            send(qo_all.at[t], qo_all.at[t], qo_fs.at[t], qo_rs.at[t], {"seq": mate})

        @pl.when(z - k >= 0)
        def _():
            score(s - 2 * k)

        return carry

    lax.fori_loop(1, Z, take_direct, 0)

    @pl.when(qo_bound)
    def _():
        wait_kv(s + 1)
        score(s + 1)

    def take_mate(k, carry):
        @pl.when(z - k >= 0)
        def _():
            t = mate - 2 * k
            wait_kv(t)
            score(t)

        return carry

    lax.fori_loop(1, Z, take_mate, 0)

    last = jnp.minimum(s + 2, S)
    rs_s[...] = jnp.zeros_like(rs_s)
    acc_s[...] = jnp.zeros_like(acc_s)

    def forward(t, carry):
        unnorm = jnp.exp(p_all[t] - mx_s[...])
        p_all[t] = unnorm
        rs_s[...] += jnp.sum(unnorm, axis=-1, keepdims=True)
        acc_s[...] += dot_nn(unnorm.astype(BF16), kv_all[t, :, hd:])
        return carry

    lax.fori_loop(0, last, forward, 0)
    inv_sum = 1.0 / rs_s[...]
    heads_out = (acc_s[...] / rs_s[...]).astype(BF16)
    ho_all[m] = heads_out
    out_dot = jnp.sum(upstream.astype(F32) * heads_out.astype(F32), axis=-1, keepdims=True)
    stats_all[s] = jnp.concatenate(
        [to_row(mx_s[...]), to_row(inv_sum), to_row(out_dot), jnp.zeros((5, rows), F32)], axis=0
    )
    for t in range(S):
        @pl.when((t <= s + 1) & (t != s))
        def _():
            send(stats_all.at[s], stats_all.at[s], st_ss.at[t], st_rs.at[s], {"seq": jnp.int32(t)})
    for k in range(1, M):
        to = lax.rem(m + k, M)
        send(ho_all.at[m], ho_all.at[m], ho_ss.at[to], ho_rs.at[m], {"mp": to})

    acc_s[...] = jnp.zeros_like(acc_s)

    def back_query(t, carry):
        probs = p_all[t] * inv_sum
        grad_probs = dot_nt(upstream, kv_all[t, :, hd:])
        grad_logits = (probs * (grad_probs - out_dot)).astype(BF16)
        acc_s[...] += dot_nn(grad_logits, kv_all[t, :, :hd])
        return carry

    lax.fori_loop(0, last, back_query, 0)

    dk_s[...] = jnp.zeros_like(dk_s)
    dv_s[...] = jnp.zeros_like(dv_s)
    own_place = s * rows + lax.broadcasted_iota(jnp.int32, (rows, 1), 0)

    def back_key(t, carry):
        @pl.when((t != s) & jnp.logical_not((lax.rem(t, 2) == c) & (lax.div(t, 2) > z)))
        def _():
            wait_qo(t)

        @pl.when(t != s)
        def _():
            arrived(stats_all.at[t], st_ss.at[t], st_rs.at[t], {"seq": t})

        stats = stats_all[t]
        allowed = (own_group <= group_ref[t].astype(F32)) & (own_place < clip_length)
        logits = dot_nt(kv_all[s, :, :hd], qo_all[t, :, :hd]) * factor
        probs = jnp.exp(jnp.where(allowed, logits, NEG_FILL) - stats[0:1]) * stats[1:2]
        grad_probs = dot_nt(kv_all[s, :, hd:], qo_all[t, :, hd:])
        grad_logits = (probs * (grad_probs - stats[2:3])).astype(BF16)
        dk_s[...] += dot_nn(grad_logits, qo_all[t, :, :hd])
        dv_s[...] += dot_nn(probs.astype(BF16), qo_all[t, :, hd:])
        return carry

    lax.fori_loop(jnp.maximum(s - 1, 0), S, back_key, 0)
    grad_query = norm_back(query_raw, query_inv, q_gain, acc_s[...] * factor)
    grad_key = norm_back(key_raw, key_inv, k_gain, dk_s[...] * factor)
    grad_proj = jnp.concatenate([grad_query, grad_key, dv_s[...]], axis=1).astype(BF16)

    def give_gh(k, carry):
        to = lax.rem(m + k, M)
        gh_send[to] = dot_nt(grad_proj, wq_ref[to]).astype(BF16)
        send(gh_send.at[to], gh_recv.at[m], gh_ss.at[to], gh_rs.at[m], {"mp": to})
        return carry

    lax.fori_loop(1, M, give_gh, 0)

    mine = pl.multiple_of(c * 2 * piece, 8)
    theirs = pl.multiple_of((1 - c) * 2 * piece, 8)

    def give_core(k, carry):
        at = lax.rem(z + k, Z)
        gw_s[:, :3 * hd] = dot_tn(hid_all[at], grad_proj)
        gw_s[:, 3 * hd:] = dot_tn(ga_all[at], heads_out)
        half[at] = gw_s[pl.ds(mine, 2 * piece), :]
        cx_send[at] = gw_s[pl.ds(theirs, 2 * piece), :].astype(BF16)
        send(cx_send.at[at], cx_recv.at[at], cx_ss.at[at], cx_rs.at[at], {"seq": mate})
        return carry

    lax.fori_loop(1, Z + 1, give_core, 0)

    def give_clip(k, carry):
        at = lax.rem(z + k, Z)
        arrived(cx_recv.at[at], cx_ss.at[at], cx_rs.at[at], {"seq": mate})
        both = half[at] + cx_recv[at].astype(F32)
        first, second = both[:piece], both[piece:]
        quarter[at] = jnp.where(d == 0, first, second)
        dx_send[at] = jnp.where(d == 0, second, first).astype(BF16)
        send(dx_send.at[at], dx_recv.at[at], dx_ss.at[at], dx_rs.at[at], {"dp": other_d})
        return carry

    lax.fori_loop(1, Z + 1, give_clip, 0)

    def give_z(k, carry):
        at = lax.rem(z + k, Z)
        arrived(dx_recv.at[at], dx_ss.at[at], dx_rs.at[at], {"dp": other_d})
        both = quarter[at] + dx_recv[at].astype(F32)
        quarter[at] = both

        @pl.when(k < Z)
        def _():
            zs_send[at] = both.astype(BF16)
            send(zs_send.at[at], zs_recv.at[z], zs_ss.at[at], zs_rs.at[z], {"seq": at * 2 + c})

        return carry

    lax.fori_loop(1, Z + 1, give_z, 0)

    acc_mixed = dot_nn(ho_all[m], wo_recv[m])
    go_mixed = acc_mixed
    for k in range(1, M):
        at = lax.rem(m + k, M)
        arrived(ho_all.at[at], ho_ss.at[at], ho_rs.at[at], {"mp": at})
        arrived(wo_recv.at[at], wo_ss.at[at], wo_rs.at[at], {"mp": at})
        go_mixed = go_mixed + dot_nn(ho_all[at], wo_recv[at])
    mixed_ref[...] = (lat_ref[...].astype(F32) + gate_s[...] * go_mixed).astype(BF16)

    grad_full = dot_nt(grad_proj, wq_ref[m])
    for k in range(1, M):
        at = lax.rem(m + k, M)
        arrived(gh_recv.at[at], gh_ss.at[at], gh_rs.at[at], {"mp": at})
        grad_full = grad_full + gh_recv[at].astype(F32)
    grad_normed = grad_full * (1.0 + scale_s[...])
    inner = to_row(jnp.sum(grad_normed * normed_s[...], axis=1, keepdims=True))
    dot_all[m] = jnp.broadcast_to(inner, (8, rows))
    for k in range(1, M):
        to = lax.rem(m + k, M)
        send(dot_all.at[m], dot_all.at[m], dot_ss.at[to], dot_rs.at[m], {"mp": to})

    weight = quarter[z]
    for k in range(1, Z):
        at = lax.rem(z + k, Z)
        arrived(zs_recv.at[at], zs_ss.at[at], zs_rs.at[at], {"seq": at * 2 + c})
        weight = weight + zs_recv[at].astype(F32)
    gwq_ref[...] = weight[:, :3 * hd]
    gwo_ref[...] = weight[:, 3 * hd:]

    for k in range(1, M):
        at = lax.rem(m + k, M)
        arrived(dot_all.at[at], dot_ss.at[at], dot_rs.at[at], {"mp": at})
    total = dot_all[0, 0:1, :]
    for k in range(1, M):
        total = total + dot_all[k, 0:1, :]
    mean_col = to_col(total * (1.0 / (M * width)))
    grad_inputs = inv_col * (grad_normed - normed_s[...] * mean_col)
    gl_ref[...] = (go_ref[...].astype(F32) + grad_inputs).astype(BF16)

    drained(tail_ref, prev_sem.at[0], prev_sem.at[1], after)

    def drain_mp(k, carry):
        to = lax.rem(m + k, M)
        there = {"mp": to}
        drained(ssq_all.at[m], ssq_ss.at[to], ssq_rs.at[m], there)
        drained(ga_all.at[m], ga_ss.at[to], ga_rs.at[m], there)
        drained(hid_all.at[m], hid_ss.at[to], hid_rs.at[m], there)
        drained(wo_ref.at[to], wo_ss.at[to], wo_rs.at[m], there)
        drained(ho_all.at[m], ho_ss.at[to], ho_rs.at[m], there)
        drained(gh_send.at[to], gh_ss.at[to], gh_rs.at[m], there)
        drained(dot_all.at[m], dot_ss.at[to], dot_rs.at[m], there)
        return carry

    lax.fori_loop(1, M, drain_mp, 0)

    def kv_left(t):
        drained(kv_all.at[s], kv_ss.at[t], kv_rs.at[s], {"seq": t})

    def qo_left(t):
        drained(qo_all.at[s], qo_ss.at[t], qo_rs.at[s], {"seq": t})

    kv_left(mate)
    qo_left(mate)

    @pl.when(kv_bound)
    def _():
        kv_left(s - 1)

    @pl.when(qo_bound)
    def _():
        qo_left(s + 1)

    def drain_seq(k, carry):
        @pl.when(z + k < Z)
        def _():
            t = s + 2 * k
            kv_left(t)
            drained(qo_all.at[t], qo_fs.at[t], qo_rs.at[t], {"seq": mate})

        @pl.when(z - k >= 0)
        def _():
            t = s - 2 * k
            qo_left(t)
            drained(kv_all.at[t], kv_fs.at[t], kv_rs.at[t], {"seq": mate})

        at = lax.rem(z + k, Z)
        drained(zs_send.at[at], zs_ss.at[at], zs_rs.at[z], {"seq": at * 2 + c})
        return carry

    lax.fori_loop(1, Z, drain_seq, 0)

    def drain_weights(at, carry):
        drained(cx_send.at[at], cx_ss.at[at], cx_rs.at[at], {"seq": mate})
        drained(dx_send.at[at], dx_ss.at[at], dx_rs.at[at], {"dp": other_d})
        return carry

    lax.fori_loop(0, Z, drain_weights, 0)

    def drain_stats(t, carry):
        @pl.when(t != s)
        def _():
            drained(stats_all.at[s], st_ss.at[t], st_rs.at[s], {"seq": t})

        return carry

    lax.fori_loop(0, last, drain_stats, 0)


def on_device(S, M, latents, grad_out, sync_mod, w_qkv, w_out, q_gain, k_gain, frame_of, group_id, clip_len):
    _, rows, width = latents.shape
    frames = sync_mod.shape[1]
    model_width = sync_mod.shape[2] // 2
    hd = q_gain.shape[1]
    Z = S // 2
    piece = width // 4
    m = lax.axis_index("mp")
    scale_cols = lax.dynamic_slice(sync_mod[0], (0, m * width), (frames, width))
    gate_cols = lax.dynamic_slice(sync_mod[0], (0, model_width + m * width), (frames, width))
    own_rows = -(-frames // 16) * 16
    side = 256 - width
    window = jnp.concatenate(
        [jnp.pad(scale_cols, ((0, 0), (0, side))), jnp.pad(gate_cols, ((0, 0), (0, side)))], axis=1
    )
    tail = window[frames - TAIL:]
    window = jnp.pad(window, ((0, own_rows - frames), (0, 0)))
    wq_parts = w_qkv.reshape(M, width, 3 * hd)
    wo_parts = jnp.transpose(w_out.reshape(hd, M, width), (1, 0, 2))
    vmem = pl.BlockSpec(memory_space=pltpu.VMEM)

    def buf(shape, dtype=BF16):
        return pltpu.VMEM(shape, dtype)

    def sems(*counts):
        return [pltpu.SemaphoreType.DMA((n,)) for n in counts]

    scratch = [
        buf((TAIL, 512)), buf((M, rows, width)), buf((M, rows, width)), buf((M, 8, rows), F32),
        buf((S, rows, 2 * hd)), buf((S, rows, 2 * hd)), buf((S, rows, rows), F32), buf((S, 8, rows), F32),
        buf((M, rows, hd)), buf((M, hd, width)),
        buf((M, rows, width)), buf((M, rows, width)), buf((M, 8, rows), F32),
        buf((Z, 2 * piece, 4 * hd)), buf((Z, 2 * piece, 4 * hd)), buf((Z, 2 * piece, 4 * hd), F32),
        buf((Z, piece, 4 * hd)), buf((Z, piece, 4 * hd)), buf((Z, piece, 4 * hd), F32),
        buf((Z, piece, 4 * hd)), buf((Z, piece, 4 * hd)),
        buf((rows, 3 * hd), F32), buf((rows, width), F32), buf((rows, width), F32), buf((rows, width), F32),
        buf((rows, hd), F32), buf((rows, 1), F32), buf((rows, 1), F32), buf((rows, hd), F32),
        buf((rows, hd), F32), buf((rows, hd), F32), buf((width, 4 * hd), F32),
    ] + sems(2, M, M, M, M, M, M, S, S, S, S, S, S, S, S, M, M, M, M, M, M, M, M, Z, Z, Z, Z, Z, Z)
    mixed, grad_latents, grad_wqkv, grad_wout = pl.pallas_call(
        functools.partial(block_kernel, (S, M, frames)),
        out_shape=(
            jax.ShapeDtypeStruct((rows, width), BF16),
            jax.ShapeDtypeStruct((rows, width), BF16),
            jax.ShapeDtypeStruct((piece, 3 * hd), F32),
            jax.ShapeDtypeStruct((piece, hd), F32),
        ),
        in_specs=[vmem] * 10 + [pl.BlockSpec(memory_space=pltpu.SMEM)],
        out_specs=(vmem, vmem, vmem, vmem),
        scratch_shapes=scratch,
        compiler_params=pltpu.CompilerParams(
            collective_id=0, has_side_effects=True, vmem_limit_bytes=60 * 1024 * 1024
        ),
    )(
        latents[0], grad_out[0], window, tail, wq_parts, wo_parts, q_gain, k_gain, frame_of,
        group_id.reshape(S, 1, rows), clip_len,
    )
    return (
        mixed[None], grad_latents[None], grad_wqkv.reshape(piece, 3, hd), jnp.transpose(grad_wout),
    )


def solution(mesh):
    in_specs = (
        P("dp", "seq", "mp"),
        P("dp", "seq", "mp"),
        P("dp", "seq", None),
        P(None, None, "mp"),
        P("mp", None),
        P("mp", None),
        P("mp", None),
        P("dp", "seq"),
        P("dp", None),
        P("dp"),
    )
    out_specs = (
        P("dp", "seq", "mp"),
        P("dp", "seq", "mp"),
        P(("seq", "dp"), None, "mp"),
        P("mp", ("seq", "dp")),
    )
    return jax.shard_map(
        functools.partial(on_device, mesh.shape["seq"], mesh.shape["mp"]),
        mesh=mesh, in_specs=in_specs, out_specs=out_specs, check_vma=False,
    )
```
